128 devices in a mesh: morton: 64 (over z, x, y), help: 2 (over core).
Axes of the slice: x: 4, y: 4, z: 4, core: 2. Of those that a mesh axis runs over, the one named last changes fastest.
Arguments:
- multipoles: bfloat16 [131072, 296], P(('morton', 'help')), may hold values from -6 to 6
- sources: int32 [131072, 16], P(('morton', 'help')), may hold values from 0 to 6143, as said below
- labels: int32 [131072, 16], P(('morton', 'help')), may hold values from 0 to 16, as said below
- operators: bfloat16 [16, 296, 296], replicated, may hold values from -0.375 to 0.375
Outputs:
- locals_out: float32 [131072, 296], P(('morton', 'help'))
The draws below stay inside these ranges and needn't reach their ends.
Inputs may be any that keep to these rules, and one draw needn't show every extreme that they name: The octant named by a slot, (t // (2 * 1024) - 1) * 2 * 1024 + sources[t, j], lies between 0 and 131071. `labels`: no target names one operator in two slots; the value 16 marks an empty slot.
All inputs are finite; a program needn't handle non-finite values.
Results may differ from the reference program's by a relative error of at most 0.0003.
Values may be sent and summed in bfloat16 or wider, within the bound.
A program may use at most 64 MiB of HBM per device.

```python
import jax
import jax.numpy as jnp
from jax import lax

P_SIZE = 296
OPS = 16
SLOTS = 16
REACH = 1
BLOCK = 1024
OCT = 131072
N_HELP = 2


def draw_sources(key, part):
    group_rows = N_HELP * BLOCK
    groups = OCT // group_rows
    targets = jnp.arange(OCT, dtype=jnp.int32)
    group_index = targets // group_rows
    lowest = jnp.maximum(group_index - REACH, 0) * group_rows
    highest = (jnp.minimum(group_index + REACH, groups - 1) + 1) * group_rows
    named = jax.random.randint(key, (OCT, SLOTS), lowest[:, None], highest[:, None]).astype(jnp.int32)
    relative = named - ((group_index - REACH) * group_rows)[:, None]
    top_value = (2 * REACH + 1) * group_rows - 1
    relative = relative.at[REACH * group_rows, 0].set(top_value)
    return relative.astype(jnp.int32)


def draw_labels(key, part):
    first_key = jax.random.fold_in(key, 11)
    second_key = jax.random.fold_in(key, 12)
    scores = jax.random.randint(first_key, (OCT, OPS), 0, 1048576) * OPS + jnp.arange(OPS, dtype=jnp.int32)[None, :]
    ordering = jnp.argsort(scores, axis=1, stable=True).astype(jnp.int32)[:, :SLOTS]
    group_rows = N_HELP * BLOCK
    groups = OCT // group_rows
    group_index = jnp.arange(OCT, dtype=jnp.int32) // group_rows
    threshold = 300 + 650 * group_index // max(groups - 1, 1)
    rolled = jax.random.randint(second_key, (OCT, SLOTS), 0, 1000)
    return jnp.where(rolled < threshold[:, None], ordering, OPS).astype(jnp.int32)


def steps_of(key, extent, cuts, low, largest):
    loudness = 1.0
    for position, blocks in cuts:
        heights = jax.random.uniform(jax.random.fold_in(jax.random.fold_in(key, 6), position), (blocks,), jnp.float32, low / len(cuts), largest / len(cuts))
        loudness = loudness * jnp.repeat(jnp.exp(heights), extent[position] // blocks).reshape((-1,) + (1,) * (len(extent) - 1 - position))
    return loudness


def normal_values(key, dims, scale, most, shards=(), held_as=jnp.bfloat16):
    entries = scale * jax.random.normal(key, dims, jnp.float32)
    if shards:
        entries = entries * steps_of(key, dims, shards, -0.22, 0.18)
    return jnp.clip(entries, -most, most).astype(held_as)


def setup_inputs(seed: int = 0) -> dict:
    key_of = jax.random.split(jax.random.key(seed), 5)
    return {
        "multipoles": normal_values(key_of[0], (OCT, P_SIZE), 1.0, 6.0, ((0, 128),)),
        "sources": draw_sources(jax.random.fold_in(key_of[4], 71), 0),
        "labels": draw_labels(jax.random.fold_in(key_of[4], 71), 0),
        "operators": normal_values(key_of[3], (OPS, P_SIZE, P_SIZE), P_SIZE ** -0.5, 0.375),
    }


def reference(multipoles, sources, labels, operators):
    total_rows = sources.shape[0]
    block_rows = min(512, total_rows)
    block_count = total_rows // block_rows
    stacked = operators.reshape(OPS * P_SIZE, P_SIZE)
    choices_range = jnp.arange(OPS, dtype=jnp.int32)
    group_rows = N_HELP * BLOCK
    targets = jnp.arange(total_rows, dtype=jnp.int32)
    starts = ((targets // group_rows - REACH) * group_rows).astype(jnp.int32)
    named = (sources + starts[:, None]).astype(jnp.int32)

    def one_block(pieces):
        indices, kinds = pieces
        picked = jnp.take(multipoles, indices, axis=0).astype(jnp.float32)
        onehot = (kinds[:, :, None] == choices_range[None, None, :]).astype(jnp.float32)
        gathered = jnp.einsum("tjk,tjp->tkp", onehot, picked).astype(jnp.bfloat16)
        return jnp.dot(gathered.reshape(block_rows, OPS * P_SIZE), stacked, preferred_element_type=jnp.float32)

    result = lax.map(one_block, (named.reshape(block_count, block_rows, SLOTS), labels.reshape(block_count, block_rows, SLOTS)))
    return result.reshape(total_rows, P_SIZE)
```

```python
import jax
import jax.numpy as jnp
from jax import lax
from jax.experimental import pallas as pl
from jax.experimental.pallas import tpu as pltpu
from jax.sharding import PartitionSpec as P

P_SIZE = 296
OPS = 16
SLOTS = 16
ROWS = 1024
LANES = 128
CHUNKS = 3
PITCH = 4
PADDED = CHUNKS * LANES
WINDOW = 6 * ROWS
EMPTY = WINDOW
GROUP = 4
TILE = 256
MESH = pl.DeviceIdType.MESH
CUTS = ((0, 128), (128, 128), (256, 40))


def translate_kernel(
    mult_ref, src_ref, lab_ref, op_ref, out_ref,
    recv, win, opraw, opt, left_g, right_g, idxv, idxs,
    own_sem, op_sem, idx_sem, send_sem, recv_sem,
):
    g = lax.axis_index("morton")
    h = lax.axis_index("help")
    count = lax.axis_size("morton")
    above = (lax.rem(g + 1, count), h)
    below = (lax.rem(g + count - 1, count), h)
    sibling = (g, 1 - h)

    barrier = pltpu.get_barrier_semaphore()
    for device in (sibling, above, below):
        pl.semaphore_signal(barrier, inc=1, device_id=device, device_id_type=MESH)
    pl.semaphore_wait(barrier, 3)

    def send(kind, cut, slot, device, source):
        start, size = CUTS[cut]
        return pltpu.make_async_remote_copy(
            src_ref=source.at[pl.ds(start, size)],
            dst_ref=recv.at[slot, pl.ds(start, size)],
            send_sem=send_sem.at[kind, cut],
            recv_sem=recv_sem.at[kind, cut],
            device_id=device,
            device_id_type=MESH,
        )

    ups = [send(0, c, h, above, mult_ref) for c in range(CHUNKS)]
    downs = [send(1, c, 4 + h, below, mult_ref) for c in range(CHUNKS)]
    sides = [send(2, c, 2 + h, sibling, mult_ref) for c in range(CHUNKS)]
    lows = [send(3, c, h, sibling, recv.at[h]) for c in range(CHUNKS)]
    highs = [send(4, c, 4 + h, sibling, recv.at[4 + h]) for c in range(CHUNKS)]
    for c in range(CHUNKS):
        ups[c].start()
        downs[c].start()
    for c in range(CHUNKS):
        sides[c].start()
    own = pltpu.make_async_copy(mult_ref, recv.at[2 + h, pl.ds(0, P_SIZE)], own_sem)
    own.start()
    ops_copy = pltpu.make_async_copy(op_ref, opraw, op_sem)
    ops_copy.start()

    kinds = lax.broadcasted_iota(jnp.int32, (OPS, ROWS), 0)
    picked = jnp.full((OPS, ROWS), EMPTY * PITCH, jnp.int32)
    for j in range(SLOTS):
        hit = lab_ref[j : j + 1, :] == kinds
        picked = jnp.where(hit, src_ref[j : j + 1, :] * PITCH, picked)
    for a in range(2):
        for b in range(8):
            row = (a * 8 + b) * 8
            idxv[row : row + 8, :] = picked[8 * a : 8 * a + 8, LANES * b : LANES * b + LANES]
    idx_copy = pltpu.make_async_copy(idxv, idxs, idx_sem)
    idx_copy.start()

    win[pl.ds(WINDOW * PITCH, 8 * PITCH), :] = jnp.zeros((8 * PITCH, LANES), jnp.float32)
    pad = jnp.zeros((PADDED - P_SIZE, ROWS), jnp.bfloat16)
    for s in range(6):
        recv[s, P_SIZE:, :] = pad

    def eye(n):
        return (
            lax.broadcasted_iota(jnp.int32, (n, n), 0) == lax.broadcasted_iota(jnp.int32, (n, n), 1)
        ).astype(jnp.bfloat16)

    unit = eye(TILE)

    def place(slot, c):
        @pl.loop(0, ROWS // TILE)
        def _(b):
            first = pl.multiple_of(b * TILE, TILE)
            piece = recv[slot, pl.ds(c * LANES, LANES), pl.ds(first, TILE)]
            turned = lax.dot_general(
                unit, piece, (((1,), (1,)), ((), ())), preferred_element_type=jnp.float32
            )
            base = pl.multiple_of((slot * ROWS + first) * PITCH, TILE * PITCH)
            win[pl.ds(base + c, TILE, stride=PITCH), :] = turned

    own.wait()
    for c in range(CHUNKS):
        place(2 + h, c)

    ops_copy.wait()
    unit_op = eye(P_SIZE)
    tail = jnp.zeros((P_SIZE, PADDED - P_SIZE), jnp.bfloat16)

    @pl.loop(0, OPS)
    def _(k):
        turned = lax.dot_general(
            unit_op, opraw[k], (((1,), (1,)), ((), ())), preferred_element_type=jnp.float32
        ).astype(jnp.bfloat16)
        opt[:, pl.ds(pl.multiple_of(k * PADDED, PADDED), PADDED)] = jnp.concatenate([turned, tail], axis=1)

    for c in range(CHUNKS):
        sides[c].wait_recv()
        place(3 - h, c)
    for c in range(CHUNKS):
        ups[c].wait_recv()
        lows[c].start()
        downs[c].wait_recv()
        highs[c].start()
        place(h, c)
        place(4 + h, c)
        if c:
            lows[c - 1].wait_recv()
            place(1 - h, c - 1)
            highs[c - 1].wait_recv()
            place(5 - h, c - 1)
    lows[CHUNKS - 1].wait_recv()
    place(1 - h, CHUNKS - 1)
    highs[CHUNKS - 1].wait_recv()
    place(5 - h, CHUNKS - 1)
    idx_copy.wait()

    groups = OPS // GROUP
    halves = TILE // LANES
    steps = groups * (ROWS // TILE)
    span = LANES - (8 * (halves - 1) + GROUP - 1)

    def gather(step, into):
        n, k = step // groups, lax.rem(step, groups) * GROUP
        base = ((k // 8) * 8 + n * halves) * 8 + lax.rem(k, 8)
        for kk in range(GROUP):
            for half in range(halves):
                column = idxs.at[pl.ds(8 * half + kk, span)]
                for lane in range(LANES):
                    row = column.at[:, pl.ds(lane, 1)][base, 0]
                    to = (kk * TILE + half * LANES + lane) * PITCH
                    into[pl.ds(to, PITCH), :] = win[pl.ds(row, PITCH), :]

    def multiply(step, held):
        n, k = step // groups, lax.rem(step, groups)
        parts = []
        for kk in range(GROUP):
            for c in range(CHUNKS):
                parts.append(
                    held[pl.ds(kk * TILE * PITCH + c, TILE, stride=PITCH), :].astype(jnp.bfloat16)
                )
        depth = GROUP * PADDED
        result = lax.dot_general(
            opt[:, pl.ds(pl.multiple_of(k * depth, depth), depth)],
            jnp.concatenate(parts, axis=1),
            (((1,), (1,)), ((), ())),
            preferred_element_type=jnp.float32,
        )
        where = pl.ds(pl.multiple_of(n * TILE, TILE), TILE)
        out_ref[:, where] += result

    out_ref[...] = jnp.zeros_like(out_ref)
    gather(0, left_g)

    @pl.loop(0, steps // 2)
    def _(pair):
        step = pair * 2
        gather(step + 1, right_g)
        multiply(step, left_g)
        gather(lax.rem(step + 2, steps), left_g)
        multiply(step + 1, right_g)

    for c in range(CHUNKS):
        for copy in (ups[c], downs[c], sides[c], lows[c], highs[c]):
            copy.wait_send()


def per_device(multipoles, sources, labels, operators):
    vmem = pl.BlockSpec(memory_space=pltpu.VMEM)
    anywhere = pl.BlockSpec(memory_space=pl.ANY)
    out = pl.pallas_call(
        translate_kernel,
        out_shape=jax.ShapeDtypeStruct((P_SIZE, ROWS), jnp.float32),
        in_specs=[anywhere, vmem, vmem, anywhere],
        out_specs=vmem,
        scratch_shapes=[
            pltpu.VMEM((6, PADDED, ROWS), jnp.bfloat16),
            pltpu.VMEM(((WINDOW + 8) * PITCH, LANES), jnp.float32),
            pltpu.VMEM((OPS, P_SIZE, P_SIZE), jnp.bfloat16),
            pltpu.VMEM((P_SIZE, OPS * PADDED), jnp.bfloat16),
            pltpu.VMEM((GROUP * TILE * PITCH, LANES), jnp.float32),
            pltpu.VMEM((GROUP * TILE * PITCH, LANES), jnp.float32),
            pltpu.VMEM((LANES, LANES), jnp.int32),
            pltpu.SMEM((LANES, LANES), jnp.int32),
            pltpu.SemaphoreType.DMA,
            pltpu.SemaphoreType.DMA,
            pltpu.SemaphoreType.DMA,
            pltpu.SemaphoreType.DMA((5, CHUNKS)),
            pltpu.SemaphoreType.DMA((5, CHUNKS)),
        ],
        compiler_params=pltpu.CompilerParams(
            collective_id=0, has_side_effects=True, vmem_limit_bytes=56 * 1024 * 1024
        ),
        name="translate",
    )(multipoles.T, sources.T, labels.T, operators)
    return out.T


def solution(mesh):
    placed = (
        P(("morton", "help"), None),
        P(("morton", "help"), None),
        P(("morton", "help"), None),
        P(),
    )
    return jax.shard_map(
        per_device,
        mesh=mesh,
        in_specs=placed,
        out_specs=P(("morton", "help"), None),
        check_vma=False,
    )
```

```python
import jax
import jax.numpy as jnp
from jax import lax
from jax.experimental import pallas as pl
from jax.experimental.pallas import tpu as pltpu
from jax.sharding import PartitionSpec as P

P_SIZE = 296
OPS = 16
SLOTS = 16
ROWS = 1024
LANES = 128
CHUNKS = 3
PITCH = 4
PADDED = CHUNKS * LANES
PIECES = 4
WINDOW = 6 * ROWS
EMPTY = WINDOW
GROUP = 4
TILE = 256
MESH = pl.DeviceIdType.MESH


def translate_kernel(
    mult_ref, src_hbm, lab_hbm, op_ref, out_ref,
    recv, win, opraw, opt, left_g, right_g, src_ref, lab_ref, idxv, idxs, total,
    own_sem, src_sem, lab_sem, op_sem, idx_sem, out_sem, send_sem, recv_sem,
):
    g = lax.axis_index("morton")
    h = lax.axis_index("help")
    count = lax.axis_size("morton")
    above = (lax.rem(g + 1, count), h)
    below = (lax.rem(g + count - 1, count), h)
    sibling = (g, 1 - h)
    has_above = g < count - 1
    has_below = g > 0

    barrier = pltpu.get_barrier_semaphore()
    pl.semaphore_signal(barrier, inc=1, device_id=sibling, device_id_type=MESH)

    @pl.when(has_above)
    def _():
        pl.semaphore_signal(barrier, inc=1, device_id=above, device_id_type=MESH)

    @pl.when(has_below)
    def _():
        pl.semaphore_signal(barrier, inc=1, device_id=below, device_id_type=MESH)

    pl.semaphore_wait(barrier, 1 + has_above.astype(jnp.int32) + has_below.astype(jnp.int32))

    def lanes(b):
        return pl.ds(b * TILE, TILE)

    def send(kind, b, slot, device, source):
        return pltpu.make_async_remote_copy(
            src_ref=source.at[:, lanes(b)],
            dst_ref=recv.at[slot, pl.ds(0, P_SIZE), lanes(b)],
            send_sem=send_sem.at[kind, b],
            recv_sem=recv_sem.at[kind, b],
            device_id=device,
            device_id_type=MESH,
        )

    order = range(PIECES)
    ups = [send(0, b, h, above, mult_ref) for b in order]
    downs = [send(1, b, 4 + h, below, mult_ref) for b in order]
    sides = [send(2, b, 2 + h, sibling, mult_ref) for b in order]
    lows = [send(3, b, h, sibling, recv.at[h, pl.ds(0, P_SIZE)]) for b in order]
    highs = [send(4, b, 4 + h, sibling, recv.at[4 + h, pl.ds(0, P_SIZE)]) for b in order]
    for b in order:

        @pl.when(has_above)
        def _(b=b):
            ups[b].start()

        @pl.when(has_below)
        def _(b=b):
            downs[b].start()

    for b in order:
        sides[b].start()
    src_copy = pltpu.make_async_copy(src_hbm, src_ref, src_sem)
    lab_copy = pltpu.make_async_copy(lab_hbm, lab_ref, lab_sem)
    own = pltpu.make_async_copy(mult_ref, recv.at[2 + h, pl.ds(0, P_SIZE)], own_sem)
    ops_copy = pltpu.make_async_copy(op_ref, opraw, op_sem)
    src_copy.start()
    lab_copy.start()
    own.start()
    ops_copy.start()

    win[pl.ds(WINDOW * PITCH, 8 * PITCH), :] = jnp.zeros((8 * PITCH, LANES), jnp.float32)
    pad = jnp.zeros((PADDED - P_SIZE, ROWS), jnp.bfloat16)
    for s in range(6):
        recv[s, P_SIZE:, :] = pad

    src_copy.wait()
    lab_copy.wait()
    kinds = lax.broadcasted_iota(jnp.int32, (OPS, ROWS), 0)
    picked = jnp.full((OPS, ROWS), EMPTY * PITCH, jnp.int32)
    for j in range(SLOTS):
        hit = lab_ref[j : j + 1, :] == kinds
        picked = jnp.where(hit, src_ref[j : j + 1, :] * PITCH, picked)
    for a in range(2):
        for b in range(8):
            row = (a * 8 + b) * 8
            idxv[row : row + 8, :] = picked[8 * a : 8 * a + 8, LANES * b : LANES * b + LANES]
    idx_copy = pltpu.make_async_copy(idxv, idxs, idx_sem)
    idx_copy.start()

    def eye(n):
        return (
            lax.broadcasted_iota(jnp.int32, (n, n), 0) == lax.broadcasted_iota(jnp.int32, (n, n), 1)
        ).astype(jnp.bfloat16)

    unit = eye(TILE)

    def place(pairs):
        for slot, b in pairs:
            turned = lax.dot_general(
                unit, recv[slot, :, lanes(b)], (((1,), (1,)), ((), ())), preferred_element_type=jnp.float32
            )
            base = pl.multiple_of((slot * ROWS + b * TILE) * PITCH, TILE * PITCH)
            for c in range(CHUNKS):
                win[pl.ds(base + c, TILE, stride=PITCH), :] = turned[:, c * LANES : c * LANES + LANES]

    ops_copy.wait()
    unit_op = eye(P_SIZE)
    tail = jnp.zeros((P_SIZE, PADDED - P_SIZE), jnp.bfloat16)

    @pl.loop(0, OPS)
    def _(k):
        turned = lax.dot_general(
            unit_op, opraw[k], (((1,), (1,)), ((), ())), preferred_element_type=jnp.float32
        ).astype(jnp.bfloat16)
        opt[:, pl.ds(pl.multiple_of(k * PADDED, PADDED), PADDED)] = jnp.concatenate([turned, tail], axis=1)

    own.wait()
    place([(2 + h, b) for b in order])
    for b in order:
        sides[b].wait_recv()
    place([(3 - h, b) for b in order])

    def receive(b):
        @pl.when(has_below)
        def _():
            ups[b].wait_recv()
            lows[b].start()

        @pl.when(has_above)
        def _():
            downs[b].wait_recv()
            highs[b].start()

    def receive_from_sibling(b):
        @pl.when(has_below)
        def _():
            lows[b].wait_recv()

        @pl.when(has_above)
        def _():
            highs[b].wait_recv()

    for b in order:
        receive(b)
        if b:
            receive_from_sibling(b - 1)
            place([(h, b), (4 + h, b), (1 - h, b - 1), (5 - h, b - 1)])
        else:
            place([(h, b), (4 + h, b)])
    receive_from_sibling(PIECES - 1)
    place([(1 - h, PIECES - 1), (5 - h, PIECES - 1)])
    idx_copy.wait()

    groups = OPS // GROUP
    blocks = ROWS // TILE
    halves = TILE // LANES
    span = LANES - (8 * (halves - 1) + GROUP - 1)
    depth = GROUP * PADDED

    def gather(n, k, into):
        base = ((k * GROUP // 8) * 8 + n * halves) * 8 + k * GROUP % 8
        for kk in range(GROUP):
            for half in range(halves):
                column = idxs.at[pl.ds(8 * half + kk, span)]
                for lane in range(LANES):
                    row = column.at[:, pl.ds(lane, 1)][base, 0]
                    to = (kk * TILE + half * LANES + lane) * PITCH
                    into[pl.ds(to, PITCH), :] = win[pl.ds(row, PITCH), :]

    def multiply(n, k, held):
        parts = []
        for kk in range(GROUP):
            for c in range(CHUNKS):
                parts.append(
                    held[pl.ds(kk * TILE * PITCH + c, TILE, stride=PITCH), :].astype(jnp.bfloat16)
                )
        result = lax.dot_general(
            opt[:, k * depth : (k + 1) * depth],
            jnp.concatenate(parts, axis=1),
            (((1,), (1,)), ((), ())),
            preferred_element_type=jnp.float32,
        )
        where = pl.ds(pl.multiple_of(n * TILE, TILE), TILE)
        if k:
            total[:, where] += result
        else:
            total[:, where] = result

    def leave(n):
        where = pl.ds(pl.multiple_of(n * TILE, TILE), TILE)
        return pltpu.make_async_copy(total.at[:, where], out_ref.at[:, where], out_sem.at[n])

    gather(0, 0, left_g)

    @pl.loop(0, blocks)
    def _(n):
        for k in range(groups):
            held, into = (right_g, left_g) if k % 2 else (left_g, right_g)
            if k < groups - 1:
                gather(n, k + 1, into)
            else:
                gather(lax.rem(n + 1, blocks), 0, into)
            multiply(n, k, held)
        leave(n).start()

    for n in range(blocks):
        leave(n).wait()
    for b in order:
        sides[b].wait_send()

        @pl.when(has_above)
        def _(b=b):
            ups[b].wait_send()
            highs[b].wait_send()

        @pl.when(has_below)
        def _(b=b):
            downs[b].wait_send()
            lows[b].wait_send()


def per_device(multipoles, sources, labels, operators):
    anywhere = pl.BlockSpec(memory_space=pl.ANY)
    out = pl.pallas_call(
        translate_kernel,
        out_shape=jax.ShapeDtypeStruct((P_SIZE, ROWS), jnp.float32),
        in_specs=[anywhere] * 4,
        out_specs=anywhere,
        scratch_shapes=[
            pltpu.VMEM((6, PADDED, ROWS), jnp.bfloat16),
            pltpu.VMEM(((WINDOW + 8) * PITCH, LANES), jnp.float32),
            pltpu.VMEM((OPS, P_SIZE, P_SIZE), jnp.bfloat16),
            pltpu.VMEM((P_SIZE, OPS * PADDED), jnp.bfloat16),
            pltpu.VMEM((GROUP * TILE * PITCH + 8, LANES), jnp.float32),
            pltpu.VMEM((GROUP * TILE * PITCH + 8, LANES), jnp.float32),
            pltpu.VMEM((SLOTS, ROWS), jnp.int32),
            pltpu.VMEM((SLOTS, ROWS), jnp.int32),
            pltpu.VMEM((LANES, LANES), jnp.int32),
            pltpu.SMEM((LANES, LANES), jnp.int32),
            pltpu.VMEM((P_SIZE, ROWS), jnp.float32),
            pltpu.SemaphoreType.DMA,
            pltpu.SemaphoreType.DMA,
            pltpu.SemaphoreType.DMA,
            pltpu.SemaphoreType.DMA,
            pltpu.SemaphoreType.DMA,
            pltpu.SemaphoreType.DMA((PIECES,)),
            pltpu.SemaphoreType.DMA((5, PIECES)),
            pltpu.SemaphoreType.DMA((5, PIECES)),
        ],
        compiler_params=pltpu.CompilerParams(
            collective_id=0, has_side_effects=True, vmem_limit_bytes=56 * 1024 * 1024
        ),
        name="translate",
    )(multipoles.T, sources.T, labels.T, operators)
    return out.T


def solution(mesh):
    placed = (
        P(("morton", "help"), None),
        P(("morton", "help"), None),
        P(("morton", "help"), None),
        P(),
    )
    return jax.shard_map(
        per_device,
        mesh=mesh,
        in_specs=placed,
        out_specs=P(("morton", "help"), None),
        check_vma=False,
    )
```

```python
import jax
import jax.numpy as jnp
from jax import lax
from jax.experimental import pallas as pl
from jax.experimental.pallas import tpu as pltpu
from jax.sharding import PartitionSpec as P

P_SIZE = 296
OPS = 16
SLOTS = 16
ROWS = 1024
LANES = 128
CHUNKS = 3
PITCH = 4
PADDED = CHUNKS * LANES
PIECES = 4
WINDOW = 6 * ROWS
EMPTY = WINDOW
GROUP = 4
TILE = 256
MESH = pl.DeviceIdType.MESH


def translate_kernel(
    mult_ref, src_hbm, lab_hbm, op_ref, total,
    recv, win, opraw, opt, left_g, right_g, src_ref, lab_ref, idxv, idxs,
    own_sem, src_sem, lab_sem, op_sem, idx_sem, send_sem, recv_sem,
):
    g = lax.axis_index("morton")
    h = lax.axis_index("help")
    count = lax.axis_size("morton")
    above = (lax.rem(g + 1, count), h)
    below = (lax.rem(g + count - 1, count), h)
    sibling = (g, 1 - h)
    has_above = g < count - 1
    has_below = g > 0

    barrier = pltpu.get_barrier_semaphore()
    pl.semaphore_signal(barrier, inc=1, device_id=sibling, device_id_type=MESH)

    @pl.when(has_above)
    def _():
        pl.semaphore_signal(barrier, inc=1, device_id=above, device_id_type=MESH)

    @pl.when(has_below)
    def _():
        pl.semaphore_signal(barrier, inc=1, device_id=below, device_id_type=MESH)

    pl.semaphore_wait(barrier, 1 + has_above.astype(jnp.int32) + has_below.astype(jnp.int32))

    def lanes(b):
        return pl.ds(b * TILE, TILE)

    def send(kind, b, slot, device, source):
        return pltpu.make_async_remote_copy(
            src_ref=source.at[:, lanes(b)],
            dst_ref=recv.at[slot, pl.ds(0, P_SIZE), lanes(b)],
            send_sem=send_sem.at[kind, b],
            recv_sem=recv_sem.at[kind, b],
            device_id=device,
            device_id_type=MESH,
        )

    order = range(PIECES)
    ups = [send(0, b, h, above, mult_ref) for b in order]
    downs = [send(1, b, 4 + h, below, mult_ref) for b in order]
    sides = [send(2, b, 2 + h, sibling, mult_ref) for b in order]
    lows = [send(3, b, h, sibling, recv.at[h, pl.ds(0, P_SIZE)]) for b in order]
    highs = [send(4, b, 4 + h, sibling, recv.at[4 + h, pl.ds(0, P_SIZE)]) for b in order]
    for b in order:

        @pl.when(has_above)
        def _(b=b):
            ups[b].start()

        @pl.when(has_below)
        def _(b=b):
            downs[b].start()

    for b in order:
        sides[b].start()
    src_copy = pltpu.make_async_copy(src_hbm, src_ref, src_sem)
    lab_copy = pltpu.make_async_copy(lab_hbm, lab_ref, lab_sem)
    own = pltpu.make_async_copy(mult_ref, recv.at[2 + h, pl.ds(0, P_SIZE)], own_sem)
    ops_copy = pltpu.make_async_copy(op_ref, opraw, op_sem)
    src_copy.start()
    lab_copy.start()
    own.start()
    ops_copy.start()

    win[pl.ds(WINDOW * PITCH, 8 * PITCH), :] = jnp.zeros((8 * PITCH, LANES), jnp.float32)
    pad = jnp.zeros((PADDED - P_SIZE, ROWS), jnp.bfloat16)
    for s in range(6):
        recv[s, P_SIZE:, :] = pad

    src_copy.wait()
    lab_copy.wait()
    kinds = lax.broadcasted_iota(jnp.int32, (OPS, ROWS), 0)
    picked = jnp.full((OPS, ROWS), EMPTY * PITCH, jnp.int32)
    for j in range(SLOTS):
        hit = lab_ref[j : j + 1, :] == kinds
        picked = jnp.where(hit, src_ref[j : j + 1, :] * PITCH, picked)
    for a in range(2):
        for b in range(8):
            row = (a * 8 + b) * 8
            idxv[row : row + 8, :] = picked[8 * a : 8 * a + 8, LANES * b : LANES * b + LANES]
    idx_copy = pltpu.make_async_copy(idxv, idxs, idx_sem)
    idx_copy.start()

    def eye(n):
        return (
            lax.broadcasted_iota(jnp.int32, (n, n), 0) == lax.broadcasted_iota(jnp.int32, (n, n), 1)
        ).astype(jnp.bfloat16)

    unit = eye(TILE)

    def place(pairs):
        for slot, b in pairs:
            turned = lax.dot_general(
                unit, recv[slot, :, lanes(b)], (((1,), (1,)), ((), ())), preferred_element_type=jnp.float32
            )
            base = pl.multiple_of((slot * ROWS + b * TILE) * PITCH, TILE * PITCH)
            for c in range(CHUNKS):
                win[pl.ds(base + c, TILE, stride=PITCH), :] = turned[:, c * LANES : c * LANES + LANES]

    ops_copy.wait()
    unit_op = eye(P_SIZE)
    tail = jnp.zeros((P_SIZE, PADDED - P_SIZE), jnp.bfloat16)

    @pl.loop(0, OPS)
    def _(k):
        turned = lax.dot_general(
            unit_op, opraw[k], (((1,), (1,)), ((), ())), preferred_element_type=jnp.float32
        ).astype(jnp.bfloat16)
        opt[:, pl.ds(pl.multiple_of(k * PADDED, PADDED), PADDED)] = jnp.concatenate([turned, tail], axis=1)

    own.wait()
    place([(2 + h, b) for b in order])
    for b in order:
        sides[b].wait_recv()
    place([(3 - h, b) for b in order])

    def receive(b):
        @pl.when(has_below)
        def _():
            ups[b].wait_recv()
            lows[b].start()

        @pl.when(has_above)
        def _():
            downs[b].wait_recv()
            highs[b].start()

    def receive_from_sibling(b):
        @pl.when(has_below)
        def _():
            lows[b].wait_recv()

        @pl.when(has_above)
        def _():
            highs[b].wait_recv()

    for b in order:
        receive(b)
        if b:
            receive_from_sibling(b - 1)
            place([(h, b), (4 + h, b), (1 - h, b - 1), (5 - h, b - 1)])
        else:
            place([(h, b), (4 + h, b)])
    receive_from_sibling(PIECES - 1)
    place([(1 - h, PIECES - 1), (5 - h, PIECES - 1)])
    idx_copy.wait()

    groups = OPS // GROUP
    blocks = ROWS // TILE
    halves = TILE // LANES
    span = LANES - (8 * (halves - 1) + GROUP - 1)
    depth = GROUP * PADDED

    def gather(n, k, into):
        base = ((k * GROUP // 8) * 8 + n * halves) * 8 + k * GROUP % 8
        for kk in range(GROUP):
            for half in range(halves):
                column = idxs.at[pl.ds(8 * half + kk, span)]
                for lane in range(LANES):
                    row = column.at[:, pl.ds(lane, 1)][base, 0]
                    to = (kk * TILE + half * LANES + lane) * PITCH
                    into[pl.ds(to, PITCH), :] = win[pl.ds(row, PITCH), :]

    def multiply(n, k, held):
        parts = []
        for kk in range(GROUP):
            for c in range(CHUNKS):
                parts.append(
                    held[pl.ds(kk * TILE * PITCH + c, TILE, stride=PITCH), :].astype(jnp.bfloat16)
                )
        result = lax.dot_general(
            opt[:, k * depth : (k + 1) * depth],
            jnp.concatenate(parts, axis=1),
            (((1,), (1,)), ((), ())),
            preferred_element_type=jnp.float32,
        )
        where = pl.ds(pl.multiple_of(n * TILE, TILE), TILE)
        if k:
            total[:, where] += result
        else:
            total[:, where] = result

    def block(n, last):
        for k in range(groups):
            held, into = (right_g, left_g) if k % 2 else (left_g, right_g)
            if k < groups - 1:
                gather(n, k + 1, into)
            elif not last:
                gather(n + 1, 0, into)
            multiply(n, k, held)

    gather(0, 0, left_g)

    @pl.loop(0, blocks - 1)
    def _(n):
        block(n, False)

    block(blocks - 1, True)

    for b in order:
        sides[b].wait_send()

        @pl.when(has_above)
        def _(b=b):
            ups[b].wait_send()
            highs[b].wait_send()

        @pl.when(has_below)
        def _(b=b):
            downs[b].wait_send()
            lows[b].wait_send()


def per_device(multipoles, sources, labels, operators):
    anywhere = pl.BlockSpec(memory_space=pl.ANY)
    out = pl.pallas_call(
        translate_kernel,
        out_shape=pltpu.VMEM((P_SIZE, ROWS), jnp.float32),
        in_specs=[anywhere] * 4,
        out_specs=pl.BlockSpec(memory_space=pltpu.VMEM),
        scratch_shapes=[
            pltpu.VMEM((6, PADDED, ROWS), jnp.bfloat16),
            pltpu.VMEM(((WINDOW + 8) * PITCH, LANES), jnp.float32),
            pltpu.VMEM((OPS, P_SIZE, P_SIZE), jnp.bfloat16),
            pltpu.VMEM((P_SIZE, OPS * PADDED), jnp.bfloat16),
            pltpu.VMEM((GROUP * TILE * PITCH + 8, LANES), jnp.float32),
            pltpu.VMEM((GROUP * TILE * PITCH + 8, LANES), jnp.float32),
            pltpu.VMEM((SLOTS, ROWS), jnp.int32),
            pltpu.VMEM((SLOTS, ROWS), jnp.int32),
            pltpu.VMEM((LANES, LANES), jnp.int32),
            pltpu.SMEM((LANES, LANES), jnp.int32),
            pltpu.SemaphoreType.DMA,
            pltpu.SemaphoreType.DMA,
            pltpu.SemaphoreType.DMA,
            pltpu.SemaphoreType.DMA,
            pltpu.SemaphoreType.DMA,
            pltpu.SemaphoreType.DMA((5, PIECES)),
            pltpu.SemaphoreType.DMA((5, PIECES)),
        ],
        compiler_params=pltpu.CompilerParams(
            collective_id=0, has_side_effects=True, vmem_limit_bytes=58 * 1024 * 1024
        ),
        name="translate",
    )(multipoles.T, sources.T, labels.T, operators)
    return out.T


def solution(mesh):
    placed = (
        P(("morton", "help"), None),
        P(("morton", "help"), None),
        P(("morton", "help"), None),
        P(),
    )
    return jax.shard_map(
        per_device,
        mesh=mesh,
        in_specs=placed,
        out_specs=P(("morton", "help"), None),
        check_vma=False,
    )
```

```python
import jax
import jax.numpy as jnp
from jax import lax
from jax.experimental import pallas as pl
from jax.experimental.pallas import tpu as pltpu
from jax.sharding import PartitionSpec as P

P_SIZE = 296
OPS = 16
SLOTS = 16
ROWS = 1024
LANES = 128
CHUNKS = 3
PITCH = 4
PADDED = CHUNKS * LANES
CUTS = ((0, 256), (256, 256), (512, 256), (768, 128), (896, 128))
PIECES = len(CUTS)
WINDOW = 6 * ROWS
EMPTY = WINDOW
GROUP = 4
TILE = 256
MESH = pl.DeviceIdType.MESH


def translate_kernel(
    mult_ref, src_hbm, lab_hbm, op_ref, total,
    recv, win, opraw, opt, left_g, right_g, src_ref, lab_ref, idxv, idxs,
    own_sem, src_sem, lab_sem, op_sem, idx_sem, send_sem, recv_sem,
):
    g = lax.axis_index("morton")
    h = lax.axis_index("help")
    count = lax.axis_size("morton")
    above = (lax.rem(g + 1, count), h)
    below = (lax.rem(g + count - 1, count), h)
    sibling = (g, 1 - h)
    has_above = g < count - 1
    has_below = g > 0

    barrier = pltpu.get_barrier_semaphore()
    pl.semaphore_signal(barrier, inc=1, device_id=sibling, device_id_type=MESH)

    @pl.when(has_above)
    def _():
        pl.semaphore_signal(barrier, inc=1, device_id=above, device_id_type=MESH)

    @pl.when(has_below)
    def _():
        pl.semaphore_signal(barrier, inc=1, device_id=below, device_id_type=MESH)

    pl.semaphore_wait(barrier, 1 + has_above.astype(jnp.int32) + has_below.astype(jnp.int32))

    def lanes(b):
        return pl.ds(*CUTS[b])

    def send(kind, b, slot, device, source):
        return pltpu.make_async_remote_copy(
            src_ref=source.at[:, lanes(b)],
            dst_ref=recv.at[slot, pl.ds(0, P_SIZE), lanes(b)],
            send_sem=send_sem.at[kind, b],
            recv_sem=recv_sem.at[kind, b],
            device_id=device,
            device_id_type=MESH,
        )

    order = range(PIECES)
    ups = [send(0, b, h, above, mult_ref) for b in order]
    downs = [send(1, b, 4 + h, below, mult_ref) for b in order]
    sides = [send(2, b, 2 + h, sibling, mult_ref) for b in order]
    lows = [send(3, b, h, sibling, recv.at[h, pl.ds(0, P_SIZE)]) for b in order]
    highs = [send(4, b, 4 + h, sibling, recv.at[4 + h, pl.ds(0, P_SIZE)]) for b in order]
    for b in order:

        @pl.when(has_above)
        def _(b=b):
            ups[b].start()

        @pl.when(has_below)
        def _(b=b):
            downs[b].start()

    for b in order:
        sides[b].start()
    src_copy = pltpu.make_async_copy(src_hbm, src_ref, src_sem)
    lab_copy = pltpu.make_async_copy(lab_hbm, lab_ref, lab_sem)
    own = pltpu.make_async_copy(mult_ref, recv.at[2 + h, pl.ds(0, P_SIZE)], own_sem)
    ops_copy = pltpu.make_async_copy(op_ref, opraw, op_sem)
    src_copy.start()
    lab_copy.start()
    own.start()
    ops_copy.start()

    win[pl.ds(WINDOW * PITCH, 8 * PITCH), :] = jnp.zeros((8 * PITCH, LANES), jnp.float32)
    pad = jnp.zeros((PADDED - P_SIZE, ROWS), jnp.bfloat16)
    for s in range(6):
        recv[s, P_SIZE:, :] = pad

    src_copy.wait()
    lab_copy.wait()
    kinds = lax.broadcasted_iota(jnp.int32, (OPS, ROWS), 0)
    picked = jnp.full((OPS, ROWS), EMPTY * PITCH, jnp.int32)
    for j in range(SLOTS):
        hit = lab_ref[j : j + 1, :] == kinds
        picked = jnp.where(hit, src_ref[j : j + 1, :] * PITCH, picked)
    for a in range(2):
        for b in range(8):
            row = (a * 8 + b) * 8
            idxv[row : row + 8, :] = picked[8 * a : 8 * a + 8, LANES * b : LANES * b + LANES]
    idx_copy = pltpu.make_async_copy(idxv, idxs, idx_sem)
    idx_copy.start()

    def eye(n):
        return (
            lax.broadcasted_iota(jnp.int32, (n, n), 0) == lax.broadcasted_iota(jnp.int32, (n, n), 1)
        ).astype(jnp.bfloat16)

    unit = eye(TILE)

    def place(pairs):
        for slot, b in pairs:
            start, size = CUTS[b]
            turned = lax.dot_general(
                unit[:size, :size],
                recv[slot, :, lanes(b)],
                (((1,), (1,)), ((), ())),
                preferred_element_type=jnp.float32,
            )
            base = pl.multiple_of((slot * ROWS + start) * PITCH, LANES * PITCH)
            for c in range(CHUNKS):
                win[pl.ds(base + c, size, stride=PITCH), :] = turned[:, c * LANES : c * LANES + LANES]

    ops_copy.wait()
    unit_op = eye(P_SIZE)
    tail = jnp.zeros((P_SIZE, PADDED - P_SIZE), jnp.bfloat16)

    @pl.loop(0, OPS)
    def _(k):
        turned = lax.dot_general(
            unit_op, opraw[k], (((1,), (1,)), ((), ())), preferred_element_type=jnp.float32
        ).astype(jnp.bfloat16)
        opt[:, pl.ds(pl.multiple_of(k * PADDED, PADDED), PADDED)] = jnp.concatenate([turned, tail], axis=1)

    own.wait()
    place([(2 + h, b) for b in order])
    for b in order:
        sides[b].wait_recv()
    place([(3 - h, b) for b in order])

    def receive(b):
        @pl.when(has_below)
        def _():
            ups[b].wait_recv()
            lows[b].start()

        @pl.when(has_above)
        def _():
            downs[b].wait_recv()
            highs[b].start()

    def receive_from_sibling(b):
        @pl.when(has_below)
        def _():
            lows[b].wait_recv()

        @pl.when(has_above)
        def _():
            highs[b].wait_recv()

    for b in order:
        receive(b)
        if b:
            receive_from_sibling(b - 1)
            place([(h, b), (4 + h, b), (1 - h, b - 1), (5 - h, b - 1)])
        else:
            place([(h, b), (4 + h, b)])
    receive_from_sibling(PIECES - 1)
    place([(1 - h, PIECES - 1), (5 - h, PIECES - 1)])
    idx_copy.wait()

    groups = OPS // GROUP
    blocks = ROWS // TILE
    halves = TILE // LANES
    span = LANES - (8 * (halves - 1) + GROUP - 1)
    depth = GROUP * PADDED

    def gather(n, k, into):
        base = ((k * GROUP // 8) * 8 + n * halves) * 8 + k * GROUP % 8
        for kk in range(GROUP):
            for half in range(halves):
                column = idxs.at[pl.ds(8 * half + kk, span)]
                for lane in range(LANES):
                    row = column.at[:, pl.ds(lane, 1)][base, 0]
                    to = (kk * TILE + half * LANES + lane) * PITCH
                    into[pl.ds(to, PITCH), :] = win[pl.ds(row, PITCH), :]

    def multiply(n, k, held):
        parts = []
        for kk in range(GROUP):
            for c in range(CHUNKS):
                parts.append(
                    held[pl.ds(kk * TILE * PITCH + c, TILE, stride=PITCH), :].astype(jnp.bfloat16)
                )
        result = lax.dot_general(
            opt[:, k * depth : (k + 1) * depth],
            jnp.concatenate(parts, axis=1),
            (((1,), (1,)), ((), ())),
            preferred_element_type=jnp.float32,
        )
        where = pl.ds(pl.multiple_of(n * TILE, TILE), TILE)
        if k:
            total[:, where] += result
        else:
            total[:, where] = result

    def block(n, last):
        for k in range(groups):
            held, into = (right_g, left_g) if k % 2 else (left_g, right_g)
            if k < groups - 1:
                gather(n, k + 1, into)
            elif not last:
                gather(n + 1, 0, into)
            multiply(n, k, held)

    gather(0, 0, left_g)

    @pl.loop(0, blocks - 1)
    def _(n):
        block(n, False)

    block(blocks - 1, True)

    for b in order:
        sides[b].wait_send()

        @pl.when(has_above)
        def _(b=b):
            ups[b].wait_send()
            highs[b].wait_send()

        @pl.when(has_below)
        def _(b=b):
            downs[b].wait_send()
            lows[b].wait_send()


def per_device(multipoles, sources, labels, operators):
    anywhere = pl.BlockSpec(memory_space=pl.ANY)
    out = pl.pallas_call(
        translate_kernel,
        out_shape=pltpu.VMEM((P_SIZE, ROWS), jnp.float32),
        in_specs=[anywhere] * 4,
        out_specs=pl.BlockSpec(memory_space=pltpu.VMEM),
        scratch_shapes=[
            pltpu.VMEM((6, PADDED, ROWS), jnp.bfloat16),
            pltpu.VMEM(((WINDOW + 8) * PITCH, LANES), jnp.float32),
            pltpu.VMEM((OPS, P_SIZE, P_SIZE), jnp.bfloat16),
            pltpu.VMEM((P_SIZE, OPS * PADDED), jnp.bfloat16),
            pltpu.VMEM((GROUP * TILE * PITCH + 8, LANES), jnp.float32),
            pltpu.VMEM((GROUP * TILE * PITCH + 8, LANES), jnp.float32),
            pltpu.VMEM((SLOTS, ROWS), jnp.int32),
            pltpu.VMEM((SLOTS, ROWS), jnp.int32),
            pltpu.VMEM((LANES, LANES), jnp.int32),
            pltpu.SMEM((LANES, LANES), jnp.int32),
            pltpu.SemaphoreType.DMA,
            pltpu.SemaphoreType.DMA,
            pltpu.SemaphoreType.DMA,
            pltpu.SemaphoreType.DMA,
            pltpu.SemaphoreType.DMA,
            pltpu.SemaphoreType.DMA((5, PIECES)),
            pltpu.SemaphoreType.DMA((5, PIECES)),
        ],
        compiler_params=pltpu.CompilerParams(
            collective_id=0, has_side_effects=True, vmem_limit_bytes=58 * 1024 * 1024
        ),
        name="translate",
    )(multipoles.T, sources.T, labels.T, operators)
    return out.T


def solution(mesh):
    placed = (
        P(("morton", "help"), None),
        P(("morton", "help"), None),
        P(("morton", "help"), None),
        P(),
    )
    return jax.shard_map(
        per_device,
        mesh=mesh,
        in_specs=placed,
        out_specs=P(("morton", "help"), None),
        check_vma=False,
    )
```
